128 devices in a mesh: row: 16 (over x, z), col: 8 (over y, core).
Axes of the slice: x: 4, y: 4, z: 4, core: 2. Of those that a mesh axis runs over, the one named last changes fastest.
Arguments:
- blocks: bfloat16 [512, 16, 128, 128], P('row', 'col'), may hold values from -0.375 to 0.375
- pattern: int32 [512, 16], replicated, may hold values from 0 to 511, as said below
- owners: int32 [8, 512, 2, 1], P('col', 'row'), may hold values from 0 to 15; in each aligned block of 64 rows (0 to 63, 64 to 127, ..., all dimensions but the last counted through in order) at most 6 rows name the same one
Outputs:
- moved: bfloat16 [8, 16, 96, 128, 128], P('col', 'row')
The draws below stay inside these ranges and needn't reach their ends.
Inputs may be any that keep to these rules, and one draw needn't show every extreme that they name: `pattern`: block row i holds 16 distinct column blocks (i + d) mod 512, by rising d with |d| <= 8, d = 0 among them, in slot order. `owners`: among the 64 entries of one device no value occurs more than 6 times; in some device some value occurs exactly 6 times.
All inputs are finite; a program needn't handle non-finite values.
Results may differ from the reference program's by a relative error of at most 0.0049.
Values may be sent and summed in bfloat16 or wider, within the bound.
No kernel may reach another device: no remote copies, remote signals or barrier semaphores. Data moves between devices by JAX's collectives and lax.ppermute only.
A program may use at most 192 MiB of HBM per device.

```python
import math
import jax
import jax.numpy as jnp
import numpy as np
from jax import lax

B = 128
K = 16
RG = 32
NB = 512
W = 8
KS = 2
BLK_DEV = 64
CAP = 6
N_ROW = 16
N_COL = 8


def draw_pattern(key, part):
    dropped = jax.random.randint(jax.random.fold_in(key, 11), (NB,), 0, K, dtype=jnp.int32)
    dropped = dropped + (dropped >= W).astype(jnp.int32)
    slot_ids = jnp.arange(K, dtype=jnp.int32)[None, :]
    candidate = slot_ids + (slot_ids >= dropped[:, None]).astype(jnp.int32)
    offsets = candidate - W
    row_ids = jnp.arange(NB, dtype=jnp.int32)[:, None]
    return ((row_ids + offsets + NB) % NB).astype(jnp.int32)


def block_scale(own_key, dims, cuts, low, top_value):
    gain = 1.0
    for dim, parts in cuts:
        steps = jax.random.uniform(jax.random.fold_in(jax.random.fold_in(own_key, 6), dim), (parts,), jnp.float32, low / len(cuts), top_value / len(cuts))
        gain = gain * jnp.repeat(jnp.exp(steps), dims[dim] // parts).reshape((-1,) + (1,) * (len(dims) - 1 - dim))
    return gain


def shared_out(own_key, own, number, rows, count, top, bound, slope):
    ranking = jax.random.permutation(own_key, count)
    heavy_load, ordinary = shares(count, rows * top, bound, slope, True), shares(count, rows * top, bound, slope, False)
    places = jnp.arange(count)

    def named(lengths, turn):
        used = int((lengths > 0).sum())
        fixed = max(1, used // 4)
        passed = fixed + (places - fixed + turn * (used - fixed)) % max(1, count - fixed)
        return jnp.zeros((count,), jnp.int32).at[ranking[jnp.where(places < fixed, places, passed)]].set(jnp.asarray(lengths, jnp.int32))

    lengths = jnp.where(number % 4 == 0, named(heavy_load, number // 4), named(ordinary, number - number // 4 - 1))
    mixed = jax.random.permutation(jax.random.fold_in(own, 3), count)
    source_of, taker = mixed[0:count // 2 * 2:2], mixed[1:count // 2 * 2:2]
    margin = jnp.minimum(lengths[source_of] - 1, bound - lengths[taker]) // 2
    margin = jnp.where((source_of == ranking[0]) | (taker == ranking[0]) | (lengths[taker] == 0), 0, jnp.maximum(margin, 0))
    passed = jax.random.randint(jax.random.fold_in(own, 4), (count // 2,), 0, 1 << 20) % (margin + 1)
    lengths = lengths.at[source_of].add(-passed).at[taker].add(passed)
    members = jnp.searchsorted(jnp.cumsum(lengths), jnp.arange(rows * top), side="right").astype(jnp.int32)
    table = members.reshape(top, rows).T
    table = table[jax.random.permutation(jax.random.fold_in(own, 1), rows)]
    turn = jax.random.randint(jax.random.fold_in(own, 2), (rows, 1), 0, top)
    return jnp.take_along_axis(table, (jnp.arange(top)[None, :] + turn) % top, axis=1)


def shares(number_of, total, limit, slope, full):
    weights = [(1 << 20) // math.isqrt(grade ** slope) + 1 for grade in range(1, number_of + 1)]
    largest = limit if full else min(limit, max(-(-total // number_of), total * weights[0] // sum(weights)))
    least = 1 if total - largest >= number_of - 1 else 0
    holding, spare = [largest] + [least] * (number_of - 1), total - largest - least * (number_of - 1)
    while spare > 0:
        candidates = [i for i in range(1, number_of) if holding[i] < largest] or [i for i in range(1, number_of) if holding[i] < limit]
        mass, budget = sum([weights[i] for i in candidates]), spare
        for i in candidates:
            extra = min(limit - holding[i], max(1, budget * weights[i] // mass), spare)
            holding[i] = holding[i] + extra
            spare = spare - extra
    return np.array(holding)


def noise(key, dims, scale, reach, cuts=(), kind=jnp.bfloat16):
    entries = jax.random.normal(key, dims, jnp.float32) * scale
    if len(cuts) > 0:
        entries = block_scale(key, dims, cuts, -0.22, 0.18) * entries
    return jnp.clip(entries, min=-reach, max=reach).astype(kind)


def setup_inputs(seed: int = 0) -> dict:
    splits = jax.random.split(jax.random.key(seed), 4)
    blocks = noise(splits[0], (NB, K, B, B), 0.06, 0.375, ((0, 16), (1, 8)))
    pattern = draw_pattern(jax.random.fold_in(splits[3], 71), 0)
    owners_keys = jax.random.split(jax.random.fold_in(splits[2], 1), N_COL * NB * KS // BLK_DEV)
    owners_turns = jax.random.permutation(jax.random.fold_in(splits[2], 3), N_COL * NB * KS // BLK_DEV)
    owners = jax.vmap(lambda own, number: shared_out(jax.random.fold_in(splits[2], 2), own, number, BLK_DEV, N_ROW, 1, CAP, 2))(owners_keys, owners_turns).reshape((N_COL, NB, KS, 1))
    return {"blocks": blocks, "pattern": pattern, "owners": owners}


def pick_table(pattern):
    neighbour_cols = pattern[pattern]
    same_col = neighbour_cols[:, None, :, :] == pattern[:, :, None, None]
    has_match = jnp.any(same_col, axis=-1)
    match_slot = jnp.sum(same_col.astype(jnp.int32) * jnp.arange(K, dtype=jnp.int32), axis=-1)
    return jnp.where(has_match, pattern[:, None, :] * K + match_slot, NB * K).astype(jnp.int32)


def multiply(left, blocks, pick):
    flat_table = jnp.concatenate([blocks.reshape(NB * K, B, B), jnp.zeros((1, B, B), blocks.dtype)], axis=0)

    def per_group(operands):
        left_rows, pick_rows = operands
        picked = flat_table[pick_rows].astype(jnp.float32)
        return jnp.einsum('gtab,gstbc->gsac', left_rows.astype(jnp.float32), picked, precision=lax.Precision.HIGHEST)

    result = lax.map(per_group, (left.reshape(NB // 8, 8, K, B, B), pick.reshape(NB // 8, 8, K, K)))
    return result.reshape(NB, K, B, B)


def reference(blocks, pattern, owners):
    pick = pick_table(pattern)
    squared = multiply(blocks, blocks, pick).astype(jnp.bfloat16)
    cube_term = multiply(squared, blocks, pick)
    result = (3.0 * squared.astype(jnp.float32) - 2.0 * cube_term).astype(jnp.bfloat16)
    per_device = result.reshape(N_ROW, RG, N_COL, KS, B, B).transpose(2, 0, 1, 3, 4, 5)
    per_device = per_device.reshape(N_COL * N_ROW * BLK_DEV, B, B)
    destination = owners.reshape(N_COL, N_ROW, BLK_DEV)
    one_hot = (destination[..., None] == jnp.arange(N_ROW, dtype=jnp.int32)).astype(jnp.int32)
    bucket_rank = jnp.sum((jnp.cumsum(one_hot, axis=2) - 1) * one_hot, axis=-1).astype(jnp.int32)
    bucket_slot = destination * CAP + bucket_rank
    target = jnp.arange(N_ROW, dtype=jnp.int32)[:, None] * CAP + jnp.arange(CAP, dtype=jnp.int32)[None, :]
    slot_match = bucket_slot[:, None, :, None, :] == target[None, :, None, :, None]
    has_source = jnp.any(slot_match, axis=-1)
    source = jnp.sum(slot_match.astype(jnp.int32) * jnp.arange(BLK_DEV, dtype=jnp.int32), axis=-1)
    base_index = (jnp.arange(N_COL, dtype=jnp.int32)[:, None, None, None] * N_ROW
                  + jnp.arange(N_ROW, dtype=jnp.int32)[None, None, :, None]) * BLK_DEV
    flat_index = jnp.where(has_source, base_index + source, N_COL * N_ROW * BLK_DEV).astype(jnp.int32)
    padded = jnp.concatenate([per_device, jnp.zeros((1, B, B), per_device.dtype)], axis=0)
    return padded[flat_index].reshape(N_COL, N_ROW, N_ROW * CAP, B, B)
```

```python
import jax
import jax.numpy as jnp
from jax import lax
from jax.experimental import pallas as pl
from jax.experimental.pallas import tpu as pltpu
from jax.sharding import PartitionSpec as P

T = 128
REACH = 8
OWN = 4
SPAN = OWN + 2 * REACH
SLOTS = 16
NEAR = OWN * SLOTS
FAR = 43
CUT = NEAR - FAR


def tile_sl(k):
    return pl.ds(k * T, T)


def purify_kernel(cols, missing, core, own, before, after, far, relayed, out, band, squared, result, in_sem, out_sem):
    def fetch(ref, shift, row, slot):
        flat = (slot // 2) * (2 * OWN) + (row % OWN) * 2 + slot % 2 - shift
        dst = band.at[tile_sl(row), pl.ds(pl.multiple_of((cols[row * SLOTS + slot] + 1) * T, T), T)]
        pltpu.make_async_copy(ref.at[flat], dst, in_sem).start()

    def fetch_far(low, high):
        for row in range(4):
            for slot in range(7 - row, SLOTS):
                fetch(low, CUT, row, slot)
        for row in range(16, 20):
            for slot in range(0, 28 - row):
                fetch(high, 0, row, slot)

    for row in range(8, 12):
        for slot in range(SLOTS):
            fetch(own, 0, row, slot)
    for row in range(4, 8):
        for slot in range(7 - row, SLOTS):
            if slot >= 0:
                fetch(before, 0, row, slot)
    for row in range(12, 16):
        for slot in range(0, min(SLOTS, 28 - row)):
            fetch(after, 0, row, slot)

    @pl.when(core[0] == 0)
    def _():
        fetch_far(far, relayed)

    @pl.when(core[0] != 0)
    def _():
        fetch_far(relayed, far)

    zero = jnp.zeros((T, T), jnp.bfloat16)
    for row in range(SPAN):
        for col in range(SPAN):
            inside = abs(row // 2 - col // 2) <= 4 or 8 <= row < 12
            if abs(row - col) > REACH and inside:
                band[tile_sl(row), tile_sl(col + 1)] = zero
        spot = pl.multiple_of((missing[row] + 1) * T, T)
        band[tile_sl(row), pl.ds(spot, T)] = zero

    all_in = band.at[pl.ds(0, 264 * 8), pl.ds(0, 2048)]
    pltpu.make_async_copy(all_in, all_in, in_sem).wait()

    half = SPAN // 2
    for j in range(half):
        k0, k1 = max(0, j - 4) * 2 * T, min(half, j + 5) * 2 * T
        acc = jnp.dot(
            band[8 * T : 12 * T, T + k0 : T + k1],
            band[k0:k1, T + j * 2 * T : T + (j + 1) * 2 * T],
            preferred_element_type=jnp.float32,
        )
        squared[:, j * 2 * T : (j + 1) * 2 * T] = acc.astype(jnp.bfloat16)
    for a in range(OWN):
        for col in range(SPAN):
            if abs(col - a - REACH) > REACH:
                squared[tile_sl(a), tile_sl(col)] = zero
        squared[tile_sl(a), pl.ds(pl.multiple_of(missing[REACH + a] * T, T), T)] = zero
    for j in range(half):
        k0, k1 = max(0, j - 4) * 2 * T, min(half, j + 5) * 2 * T
        cube = jnp.dot(
            squared[:, k0:k1],
            band[k0:k1, T + j * 2 * T : T + (j + 1) * 2 * T],
            preferred_element_type=jnp.float32,
        )
        cut = slice(j * 2 * T, (j + 1) * 2 * T)
        result[:, cut] = (3.0 * squared[:, cut].astype(jnp.float32) - 2.0 * cube).astype(jnp.bfloat16)
    for a in range(OWN):
        for slot in range(SLOTS):
            flat = (slot // 2) * (2 * OWN) + a * 2 + slot % 2
            src = result.at[tile_sl(a), pl.ds(pl.multiple_of(cols[(REACH + a) * SLOTS + slot] * T, T), T)]
            pltpu.make_async_copy(src, out.at[flat], out_sem).start()
    all_out = result.at[:, pl.ds(0, 2048)]
    pltpu.make_async_copy(all_out, all_out, out_sem).wait()


def purify(cols, missing, core, own, before, after, far, relayed):
    smem = pl.BlockSpec(memory_space=pltpu.SMEM)
    hbm = pl.BlockSpec(memory_space=pl.ANY)
    return pl.pallas_call(
        purify_kernel,
        out_shape=jax.ShapeDtypeStruct((NEAR, T, T), jnp.bfloat16),
        in_specs=[smem] * 3 + [hbm] * 5,
        out_specs=hbm,
        scratch_shapes=[
            pltpu.VMEM((SPAN * T, (SPAN + 2) * T), jnp.bfloat16),
            pltpu.VMEM((OWN * T, SPAN * T), jnp.bfloat16),
            pltpu.VMEM((OWN * T, SPAN * T), jnp.bfloat16),
            pltpu.SemaphoreType.DMA,
            pltpu.SemaphoreType.DMA,
        ],
        compiler_params=pltpu.CompilerParams(vmem_limit_bytes=60 << 20),
        cost_estimate=pl.CostEstimate(flops=9_400_000_000, bytes_accessed=11_000_000, transcendentals=0),
        name="purify",
    )(cols, missing, core, own, before, after, far, relayed)


def bucket_kernel(source, blocks, out, held, in_sem, out_sem):
    count = out.shape[0]
    load = pltpu.make_async_copy(blocks, held.at[pl.ds(0, NEAR)], in_sem)
    load.start()
    held[NEAR] = jnp.zeros((T, T), jnp.bfloat16)
    load.wait()
    for k in range(count):
        pltpu.make_async_copy(held.at[source[k]], out.at[k], out_sem).start()
    pltpu.make_async_copy(out, out, out_sem).wait()


def bucket(source, blocks):
    count = source.shape[0]
    return pl.pallas_call(
        bucket_kernel,
        out_shape=jax.ShapeDtypeStruct((count, T, T), jnp.bfloat16),
        in_specs=[pl.BlockSpec(memory_space=pltpu.SMEM), pl.BlockSpec(memory_space=pl.ANY)],
        out_specs=pl.BlockSpec(memory_space=pl.ANY),
        scratch_shapes=[
            pltpu.VMEM((NEAR + 1, T, T), jnp.bfloat16),
            pltpu.SemaphoreType.DMA,
            pltpu.SemaphoreType.DMA,
        ],
        compiler_params=pltpu.CompilerParams(vmem_limit_bytes=60 << 20),
        cost_estimate=pl.CostEstimate(flops=0, bytes_accessed=7_000_000, transcendentals=0),
        name="bucket",
    )(source, blocks)


def bucket_source(owners, devices):
    count = owners.size
    capacity = 3 * count // (2 * devices)
    destination = owners.reshape(count)
    index = jnp.arange(count, dtype=jnp.int32)
    same = (destination[:, None] == destination[None, :]) & (index[None, :] < index[:, None])
    rank = jnp.sum(same.astype(jnp.int32), axis=1)
    place = destination * capacity + rank
    wanted = jnp.arange(devices * capacity, dtype=jnp.int32)
    match = place[None, :] == wanted[:, None]
    return count + jnp.sum(jnp.where(match, index[None, :] - count, 0), axis=1)


def per_device(blocks, pattern, owners):
    both = ("row", "col")
    nblk = pattern.shape[0]
    cols_n = lax.axis_size("col")
    rows_n = lax.axis_size("row")
    total = rows_n * cols_n
    c = lax.axis_index("col")
    me = lax.axis_index("row") * cols_n + c
    core = c % 2

    rows = me * OWN - REACH + jnp.arange(SPAN, dtype=jnp.int32)
    wrapped = (rows + nblk) % nblk
    offset = (pattern[wrapped] - wrapped[:, None] + REACH + nblk) % nblk - REACH
    place = jnp.arange(SPAN, dtype=jnp.int32)
    cols = (place[:, None] + offset).reshape(-1)
    missing = jnp.clip(place - jnp.sum(offset, axis=1), -1, SPAN)

    own = lax.all_to_all(blocks.reshape(cols_n, 2 * OWN, T, T), "col", split_axis=0, concat_axis=0, tiled=True)
    own = own.reshape(NEAR, T, T)
    before = lax.ppermute(own, both, [(i, (i + 1) % total) for i in range(total)])
    after = lax.ppermute(own, both, [((i + 1) % total, i) for i in range(total)])
    far_out = lax.dynamic_slice_in_dim(own, CUT * (1 - core), FAR, 0)
    far = lax.ppermute(far_out, both, [(i, (i + 2 - 4 * (i % 2)) % total) for i in range(total)])
    relay_out = jnp.where(core == 0, before[CUT:], after[:FAR])
    relayed = lax.ppermute(relay_out, both, [(i, i ^ 1) for i in range(total)])

    result = purify(cols, missing, core.reshape(1), own, before, after, far, relayed)
    mine = lax.all_to_all(result.reshape(cols_n, 2 * OWN, T, T), "col", split_axis=0, concat_axis=0, tiled=True)
    buckets = bucket(bucket_source(owners, rows_n), mine.reshape(NEAR, T, T))
    buckets = buckets.reshape(rows_n, -1, T, T)
    received = lax.all_to_all(buckets, "row", split_axis=0, concat_axis=0, tiled=True)
    return received.reshape(1, 1, -1, T, T)


def solution(mesh):
    in_specs = (P("row", "col", None, None), P(), P("col", "row", None, None))
    out_specs = P("col", "row", None, None, None)
    return jax.shard_map(per_device, mesh=mesh, in_specs=in_specs, out_specs=out_specs, check_vma=False)
```
